256 devices in a mesh: grp: 32 (over y, z), head: 8 (over x, core).
Axes of the slice: x: 4, y: 4, z: 8, core: 2. Of those that a mesh axis runs over, the one named last changes fastest.
Arguments:
- long_queries: bfloat16 [32768, 64, 128], P(('grp', 'head')), may hold values from -24 to 24
- long_pairs: bfloat16 [32768, 8, 256], P(('grp', 'head')), may hold values from -24 to 24
- short_queries: bfloat16 [32768, 64, 128], P(('grp', 'head')), may hold values from -24 to 24
- short_pairs: bfloat16 [32768, 8, 256], P(('grp', 'head')), may hold values from -24 to 24
- doc_lengths: int32 [32, 32], replicated, may hold values from 1 to 64, 1024 in all within a row
- destinations: int32 [32, 32], replicated, may hold values from 0 to 31, each once within a row
Outputs:
- long_result: bfloat16 [32768, 8192], P(('grp', 'head'))
- short_placed: bfloat16 [65536, 8192], P('grp', 'head')
The draws below stay inside these ranges and needn't reach their ends.
Inputs may be any that keep to these rules, and one draw needn't show every extreme that they name: `doc_lengths`: each row sums to 1024, and each row has a document of exactly 64 tokens. `destinations`: each row is a permutation, so every group receives exactly one short document from every group.
All inputs are finite; a program needn't handle non-finite values.
Results may differ from the reference program's by a relative error of at most 0.0047.
Values may be sent and summed in bfloat16 or wider, within the bound.
A program may use at most 128 MiB of HBM per device.

```python
import math
import jax
import jax.numpy as jnp
import numpy as np
from jax import lax

H = 64
KVH = 8
DH = 128
GROUPS = 32
LONG = 1024
SHORT = 1024
MAXDOC = 64
LONG_ROWS = 32768
SHORT_ROWS = 32768


def pair_draw(key, row_count):
    key_query, key_pair = jax.random.split(key, 2)
    queries = jax.random.normal(key_query, (row_count, H, DH), jnp.float32)
    pair_rows = jax.random.normal(key_pair, (row_count, KVH, 2 * DH), jnp.float32)
    queries = jnp.clip(queries, -24.0, 24.0).astype(jnp.bfloat16)
    pair_rows = jnp.clip(pair_rows, -24.0, 24.0).astype(jnp.bfloat16)
    return (queries, pair_rows)


def draw_long_queries(key, part):
    return pair_draw(jax.random.fold_in(key, 101), LONG_ROWS)[0]


def draw_long_pairs(key, part):
    return pair_draw(jax.random.fold_in(key, 101), LONG_ROWS)[1]


def draw_short_queries(key, part):
    return pair_draw(jax.random.fold_in(key, 202), SHORT_ROWS)[0]


def draw_short_pairs(key, part):
    return pair_draw(jax.random.fold_in(key, 202), SHORT_ROWS)[1]


def profile(count, total, bound, skew):
    weights = [(1 << 20) // math.isqrt(rank ** skew) + 1 for rank in range(2, count + 1)]
    spare, counts = total - bound - (count - 1), [1] * (count - 1)
    while spare > 0:
        free = [i for i in range(count - 1) if counts[i] < bound]
        whole, budget = sum([weights[i] for i in free]), spare
        for i in free:
            addition = min(bound - counts[i], max(1, budget * weights[i] // whole), spare)
            counts[i] = counts[i] + addition
            spare = spare - addition
    return np.array([bound] + counts)


def ragged_sizes(key, count, total, limit, slope):
    if count == 2:
        one = jax.random.randint(key, (), max(1, total - limit), min(limit, total - 1) + 1)
        return jnp.stack([one, total - one])
    sizes = jnp.asarray(profile(count, total, limit, slope), jnp.int32)
    pairs = (count - 1) // 2
    donor, taker = sizes[1:1 + 2 * pairs:2], sizes[2:2 + 2 * pairs:2]
    slack = jnp.minimum(donor - 1, limit - taker)
    moved = jax.random.randint(jax.random.fold_in(key, 1), (pairs,), 0, 1 << 20) % (slack + 1)
    sizes = sizes.at[1:1 + 2 * pairs:2].set(donor - moved).at[2:2 + 2 * pairs:2].set(taker + moved)
    return sizes[jax.random.permutation(jax.random.fold_in(key, 2), count)]


def setup_inputs(seed: int = 0) -> dict:
    key_of = jax.random.split(jax.random.key(seed), 7)
    return {
        "long_queries": draw_long_queries(jax.random.fold_in(key_of[6], 71), 0),
        "long_pairs": draw_long_pairs(jax.random.fold_in(key_of[6], 71), 0),
        "short_queries": draw_short_queries(jax.random.fold_in(key_of[6], 71), 0),
        "short_pairs": draw_short_pairs(jax.random.fold_in(key_of[6], 71), 0),
        "doc_lengths": jax.vmap(lambda own: ragged_sizes(own, GROUPS, SHORT, MAXDOC, 2))(jax.random.split(key_of[4], GROUPS)).reshape((GROUPS, GROUPS)).astype(jnp.int32),
        "destinations": jax.vmap(lambda own: jax.random.permutation(own, GROUPS))(jax.random.split(key_of[5], GROUPS)).reshape((GROUPS, GROUPS)).astype(jnp.int32),
    }


def attend_rows(queries, pair_rows, allowed):
    row_count = queries.shape[0]
    pair_heads = pair_rows.shape[1]
    head_size = queries.shape[2]
    group_size = queries.shape[1] // pair_heads
    grouped = queries.astype(jnp.float32).reshape(row_count, pair_heads, group_size, head_size)
    key_part = pair_rows[:, :, :head_size].astype(jnp.float32)
    value_part = pair_rows[:, :, head_size:].astype(jnp.float32)
    score_scale = 1.0 / math.sqrt(head_size)
    scores = jnp.einsum('qhgd,khd->hgqk', grouped, key_part) * score_scale
    scores = jnp.where(allowed[None, None], scores, -1e+30)
    row_max = lax.optimization_barrier(jnp.max(scores, axis=-1, keepdims=True))
    raised = jnp.exp(scores - row_max)
    weights = (raised / lax.optimization_barrier(jnp.sum(raised, axis=-1, keepdims=True))).astype(jnp.bfloat16)
    head_mix = jnp.einsum('hgqk,khd->qhgd', weights.astype(jnp.float32), value_part)
    return head_mix.reshape(row_count, queries.shape[1], head_size)

def long_group(packed):
    queries, pair_rows = packed
    position = jnp.arange(queries.shape[0], dtype=jnp.int32)
    allowed = position[None, :] <= position[:, None]
    return attend_rows(queries, pair_rows, allowed).astype(jnp.bfloat16)

def doc_attend(queries, pair_rows, length):
    position = jnp.arange(queries.shape[0], dtype=jnp.int32)
    allowed = (position[None, :] <= position[:, None]) & (position[None, :] < length)
    head_mix = attend_rows(queries, pair_rows, allowed)
    valid_rows = (position < length)[:, None, None]
    return jnp.where(valid_rows, head_mix, 0.0).astype(jnp.bfloat16)

def short_group(packed):
    queries, pair_rows, lengths, targets = packed
    starts = jnp.cumsum(lengths) - lengths
    position = jnp.arange(MAXDOC, dtype=jnp.int32)
    valid_rows = position[None, :] < lengths[:, None]
    row_index = jnp.where(valid_rows, starts[:, None] + position[None, :], 0).astype(jnp.int32)
    doc_out = jax.vmap(doc_attend)(queries[row_index], pair_rows[row_index], lengths)
    inverse = jnp.argsort(targets).astype(jnp.int32)
    return doc_out[inverse]

def reference(long_queries, long_pairs, short_queries, short_pairs, doc_lengths, destinations):
    long_all = lax.map(long_group, (long_queries.reshape(GROUPS, LONG, H, DH), long_pairs.reshape(GROUPS, LONG, KVH, 2 * DH)))
    long_result = long_all.reshape(GROUPS * LONG, H * DH)
    placed = lax.map(short_group, (short_queries.reshape(GROUPS, SHORT, H, DH), short_pairs.reshape(GROUPS, SHORT, KVH, 2 * DH), doc_lengths, destinations))
    short_placed = jnp.swapaxes(placed, 0, 1).reshape(GROUPS * GROUPS * MAXDOC, H * DH)
    return (long_result, short_placed)
```

```python
import functools
import math

import jax
import jax.numpy as jnp
from jax import lax
from jax.experimental import pallas as pl
from jax.experimental.pallas import tpu as pltpu
from jax.sharding import PartitionSpec as P

MESH = pl.DeviceIdType.MESH
BF16 = jnp.bfloat16
F32 = jnp.float32

NG = 32
NH = 8
TOK = 128
QH = 8
D = 128
DOC = 64
TB = 16
NB = DOC // TB
WROWS = TB * NB * (NB + 1) // 2
SLOT = WROWS + DOC
KROWS = DOC + TB
SCALE2 = math.log2(math.e) / math.sqrt(D)


def wrow(block):
    return TB * block * (block + 1) // 2


def perm_matrix():
    row = lax.broadcasted_iota(jnp.int32, (D, D), 0)
    col = lax.broadcasted_iota(jnp.int32, (D, D), 1)
    return (col == (row % QH) * TB + row // QH).astype(BF16)


def slot_weights(q, k, length, perm):
    st = lax.dot_general(k, q, (((1,), (1,)), ((), ())), preferred_element_type=F32)
    out = []
    for b in range(NB):
        keys = TB * (b + 1)
        s = st[:keys, b * D : (b + 1) * D]
        key = lax.broadcasted_iota(jnp.int32, (keys, D), 0)
        tok = TB * b + lax.broadcasted_iota(jnp.int32, (keys, D), 1) // QH
        s = jnp.where(key <= tok, s, -1e30)
        top = jnp.max(s, axis=0, keepdims=True)
        p = jnp.exp2((s - top) * SCALE2)
        inv = 1.0 / jnp.sum(p, axis=0, keepdims=True)
        inv = jnp.where(tok[:1] < length, inv, 0.0)
        w = (p * inv).astype(BF16)
        w = jnp.dot(w, perm, preferred_element_type=F32).astype(BF16)
        out.append(w)
    return out


def main_kernel(
    sq, skv, lq, lkv, tabs,
    recv_out, long_out,
    gq, gkv, send, lall, lqv, lout, otile,
    xq_send, xq_recv, xk_send, xk_recv, z_send, z_recv,
    l_send, l_recv, f_send, f_recv, loc_sem,
):
    g = lax.axis_index("grp")
    h = lax.axis_index("head")
    y, z = g // 8, g % 8
    x, core = h // 2, h % 2

    def group_at(i):
        m = i % 8
        oz = jnp.where(m % 2 == 0, m // 2 + 1, 8 - (m // 2 + 1))
        oz = jnp.where(m == 7, 0, oz)
        oy = i // 8
        return ((y + oy) % 4) * 8 + (z + oz) % 8, ((y + 4 - oy) % 4) * 8 + (z + 8 - oz) % 8

    SELF = 7

    barrier = pltpu.get_barrier_semaphore()
    for o in range(1, NH):
        pl.semaphore_signal(barrier, inc=1, device_id=(g, (h + o) % NH), device_id_type=MESH)

    @pl.loop(1, NG)
    def _(o):
        pl.semaphore_signal(barrier, inc=1, device_id=((g + o) % NG, h), device_id_type=MESH)

    own = pl.ds(pl.multiple_of(h * TOK, TOK), TOK)
    own_kv = pl.ds(h * (TOK // TB), TOK // TB)
    own_q = pltpu.make_async_copy(sq.at[:, h], gq.at[own], loc_sem.at[0])
    own_k = pltpu.make_async_copy(skv.at[h], gkv.at[own_kv], loc_sem.at[1])
    own_lq = pltpu.make_async_copy(lq, lqv, loc_sem.at[2])
    own_lk = pltpu.make_async_copy(lkv, lall.at[h], loc_sem.at[3])
    own_q.start()
    own_k.start()
    own_lq.start()
    own_lk.start()
    pl.semaphore_wait(barrier, NH - 1 + NG - 1)

    def x_copies(o):
        peer = (h + o) % NH
        return (
            pltpu.make_async_remote_copy(
                skv.at[peer], gkv.at[own_kv], xk_send.at[o], xk_recv.at[o],
                device_id=(g, peer), device_id_type=MESH),
            pltpu.make_async_remote_copy(
                sq.at[:, peer], gq.at[own], xq_send.at[o], xq_recv.at[o],
                device_id=(g, peer), device_id_type=MESH),
        )

    for o in range(1, NH):
        for copy in x_copies(o):
            copy.start()

    gq[NH * TOK :, :, :] = jnp.zeros((DOC, QH, D), BF16)
    gkv[NH * TOK // TB :] = jnp.zeros((KROWS // TB, TB, 2 * D), BF16)

    own_q.wait()
    own_k.wait()
    for o in range(1, NH):
        for copy in x_copies(o):
            copy.wait_recv()
    for o in range(1, NH):
        for copy in x_copies(o):
            copy.wait_send()

    own_lk.wait()
    partner = h + 1 - 2 * core

    def l_copy(n):
        return pltpu.make_async_remote_copy(
            lkv, lall.at[h], l_send.at[n], l_recv.at[n],
            device_id=(g, (h + 2 * n) % NH), device_id_type=MESH)

    def f_copy(n):
        src = (h + NH - 2 * n) % NH
        return pltpu.make_async_remote_copy(
            lall.at[src], lall.at[src], f_send.at[n], f_recv.at[n],
            device_id=(g, partner), device_id_type=MESH)

    l_pair = pltpu.make_async_remote_copy(
        lkv, lall.at[h], f_send.at[0], f_recv.at[0],
        device_id=(g, partner), device_id_type=MESH)
    l_pair.start()
    for n in range(1, 4):
        @pl.when(x + n < 4)
        def _(n=n):
            l_copy(n).start()

    perm = perm_matrix()

    def z_copy(i):
        to, _ = group_at(i)
        return pltpu.make_async_remote_copy(
            send.at[i], recv_out.at[g], z_send.at[i], z_recv.at[i],
            device_id=(to, h), device_id_type=MESH)

    def slot(i):
        to, _ = group_at(i)
        length = tabs[1, to]
        shift = tabs[3, to]
        q = gq[pl.ds(tabs[0, to], DOC)].astype(F32).reshape(DOC * QH, D).astype(BF16)
        kv = gkv[pl.ds(tabs[2, to], KROWS // TB)].reshape(KROWS, 2 * D)
        pick = lax.broadcasted_iota(jnp.int32, (DOC, KROWS), 0) + shift
        pick = (pick == lax.broadcasted_iota(jnp.int32, (DOC, KROWS), 1)).astype(BF16)
        kv = jnp.dot(pick, kv, preferred_element_type=F32).astype(BF16)
        k, v = kv[:, :D], kv[:, D:]
        for b, w in enumerate(slot_weights(q, k, length, perm)):
            send[i, wrow(b) : wrow(b + 1), :] = w
        send[i, WROWS:SLOT, :] = v

    own_slot = pltpu.make_async_copy(send.at[SELF], recv_out.at[g], loc_sem.at[4])

    def send_slot(i):
        @pl.when(i != SELF)
        def _():
            z_copy(i).start()

        @pl.when(i == SELF)
        def _():
            own_slot.start()

    slot(0)

    @pl.loop(1, NG)
    def _(i):
        slot(i)
        send_slot(i - 1)

    send_slot(NG - 1)

    own_lq.wait()
    for n in range(1, 4):
        @pl.when(x >= n)
        def _(n=n):
            l_copy(n).wait_recv()
            f_copy(n).start()

    l_pair.wait_recv()
    for n in range(1, 4):
        @pl.when(x >= n)
        def _(n=n):
            f_copy(n).wait_recv()

    def long_tile(i, chips):
        c, t = i // 4, i % 4
        q = lqv[pl.ds(t * 32, 32), c].astype(F32).reshape(32 * QH, D).astype(BF16)
        scores = []
        for b in range(chips + 1):
            k = lall[2 * b : 2 * b + 2, c, :, 0:D].reshape(2 * TOK, D)
            scores.append(lax.dot_general(q, k, (((1,), (1,)), ((), ())), preferred_element_type=F32))
        row = core * TOK + t * 32 + lax.broadcasted_iota(jnp.int32, (32 * QH, 2 * TOK), 0) // QH
        col = lax.broadcasted_iota(jnp.int32, (32 * QH, 2 * TOK), 1)
        scores[chips] = jnp.where(col <= row, scores[chips], -1e30)
        top = functools.reduce(jnp.maximum, scores)
        top = jnp.max(top, axis=1, keepdims=True)
        total = None
        acc = None
        for b in range(chips + 1):
            p = jnp.exp2((scores[b] - top) * SCALE2)
            total = p if total is None else total + p
            v = lall[2 * b : 2 * b + 2, c, :, D : 2 * D].reshape(2 * TOK, D)
            part = jnp.dot(p.astype(BF16), v, preferred_element_type=F32)
            acc = part if acc is None else acc + part
        total = jnp.sum(total, axis=1, keepdims=True)
        otile[...] = acc * (1.0 / total)
        for e in range(QH):
            rows = otile[pl.ds(e, 32, stride=QH), :].astype(BF16)
            lout[c, pl.ds(pl.multiple_of(t * 32, 32), 32), e * D : (e + 1) * D] = rows

    for chips in range(4):
        @pl.when(x == chips)
        def _(chips=chips):
            @pl.loop(0, 32)
            def _(i):
                long_tile(i, chips)

    def out_copy(c):
        return pltpu.make_async_copy(
            lout.at[c], long_out.at[:, pl.ds(pl.multiple_of(c * QH * D, QH * D), QH * D)], loc_sem.at[8 + c])

    for c in range(NH):
        out_copy(c).start()

    l_pair.wait_send()
    for n in range(1, 4):
        @pl.when(x + n < 4)
        def _(n=n):
            l_copy(n).wait_send()

        @pl.when(x >= n)
        def _(n=n):
            f_copy(n).wait_send()

    @pl.loop(0, NG)
    def _(i):
        @pl.when(i != SELF)
        def _():
            _, source = group_at(i)
            pltpu.make_async_remote_copy(
                send.at[i], recv_out.at[source], z_send.at[i], z_recv.at[i],
                device_id=(source, h), device_id_type=MESH).wait()

    own_slot.wait()
    for c in range(NH):
        out_copy(c).wait()


def exchange(sq, skv, lq, lkv, tabs):
    any_spec = pl.BlockSpec(memory_space=pl.ANY)
    smem = pl.BlockSpec(memory_space=pltpu.SMEM)
    dma = pltpu.SemaphoreType.DMA
    return pl.pallas_call(
        main_kernel,
        out_shape=(
            jax.ShapeDtypeStruct((NG, SLOT, D), BF16),
            jax.ShapeDtypeStruct((TOK, NH * QH * D), BF16),
        ),
        in_specs=[any_spec] * 4 + [smem],
        out_specs=(any_spec, any_spec),
        scratch_shapes=[
            pltpu.VMEM((NH * TOK + DOC, QH, D), BF16),
            pltpu.VMEM(((NH * TOK + KROWS) // TB, TB, 2 * D), BF16),
            pltpu.VMEM((NG, SLOT, D), BF16),
            pltpu.VMEM((NH, NH, TOK, 2 * D), BF16),
            pltpu.VMEM((TOK, NH, QH, D), BF16),
            pltpu.VMEM((NH, TOK, QH * D), BF16),
            pltpu.VMEM((32 * QH, D), F32),
            dma((NH,)), dma((NH,)), dma((NH,)), dma((NH,)),
            dma((NG,)), dma((NG,)),
            dma((4,)), dma((4,)), dma((4,)), dma((4,)),
            dma((16,)),
        ],
        compiler_params=pltpu.CompilerParams(collective_id=0, has_side_effects=True),
        name="exchange",
    )(sq, skv, lq, lkv, tabs)


def place_kernel(per_step, got, long_in, short_out, long_out):
    long_out[...] = long_in[...]
    for s in range(per_step):
        v = got[s, WROWS:SLOT, :]
        for b in range(NB):
            w = got[s, wrow(b) : wrow(b + 1), :]
            o = lax.dot_general(w, v[: TB * (b + 1)], (((0,), (0,)), ((), ())), preferred_element_type=F32)
            o = o.astype(BF16)
            at = s * DOC + b * TB
            for e in range(QH):
                short_out[at : at + TB, e * D : (e + 1) * D] = o[e * TB : (e + 1) * TB, :]


def place(got, long_in):
    per_step = 4
    steps = NG // per_step
    return pl.pallas_call(
        functools.partial(place_kernel, per_step),
        grid=(steps,),
        out_shape=(
            jax.ShapeDtypeStruct((NG * DOC, QH * D), BF16),
            jax.ShapeDtypeStruct((TOK, NH * QH * D), BF16),
        ),
        in_specs=[
            pl.BlockSpec((per_step, SLOT, D), lambda i: (i, 0, 0)),
            pl.BlockSpec((TOK // steps, NH * QH * D), lambda i: (i, 0)),
        ],
        out_specs=(
            pl.BlockSpec((per_step * DOC, QH * D), lambda i: (i, 0)),
            pl.BlockSpec((TOK // steps, NH * QH * D), lambda i: (i, 0)),
        ),
        name="place",
    )(got, long_in)


def slot_tables(doc_lengths, destinations):
    g = lax.axis_index("grp")
    lens = lax.dynamic_index_in_dim(doc_lengths, g, 0, keepdims=False)
    dest = lax.dynamic_index_in_dim(destinations, g, 0, keepdims=False)
    doc = jnp.arange(NG, dtype=jnp.int32)
    hit = dest[None, :] == doc[:, None]
    before = jnp.where(doc[None, :] < doc[:, None], lens[None, :], 0).sum(axis=1)
    start = jnp.where(hit, before[None, :], 0).sum(axis=1)
    rows = jnp.where(hit, lens[None, :], 0).sum(axis=1)
    return jnp.stack([start, rows, start // TB, start % TB])


def on_device(long_queries, long_pairs, short_queries, short_pairs, doc_lengths, destinations):
    split = (TOK, NH, QH, D)
    got, long_mix = exchange(
        short_queries.reshape(split),
        jnp.transpose(short_pairs, (1, 0, 2)).reshape(NH, TOK // TB, TB, 2 * D),
        long_queries.reshape(split),
        jnp.transpose(long_pairs, (1, 0, 2)),
        slot_tables(doc_lengths, destinations),
    )
    short_placed, long_result = place(got, long_mix)
    return long_result, short_placed


def solution(mesh):
    rows = P(("grp", "head"), None, None)
    return jax.shard_map(
        on_device,
        mesh=mesh,
        in_specs=(rows, rows, rows, rows, P(), P()),
        out_specs=(P(("grp", "head"), None), P("grp", "head")),
        check_vma=False,
    )
```

```python
import functools
import math

import jax
import jax.numpy as jnp
from jax import lax
from jax.experimental import pallas as pl
from jax.experimental.pallas import tpu as pltpu
from jax.sharding import PartitionSpec as P

MESH = pl.DeviceIdType.MESH
BF16 = jnp.bfloat16
F32 = jnp.float32

NG = 32
NH = 8
TOK = 128
QH = 8
D = 128
DOC = 64
TB = 16
NB = DOC // TB
WROWS = TB * NB * (NB + 1) // 2
SLOT = WROWS + DOC
KROWS = DOC + TB
SCALE2 = math.log2(math.e) / math.sqrt(D)


def wrow(block):
    return TB * block * (block + 1) // 2


def perm_matrix():
    row = lax.broadcasted_iota(jnp.int32, (D, D), 0)
    col = lax.broadcasted_iota(jnp.int32, (D, D), 1)
    return (col == (row % QH) * TB + row // QH).astype(BF16)


def slot_weights(q, k, length, perm):
    st = lax.dot_general(k, q, (((1,), (1,)), ((), ())), preferred_element_type=F32)
    out = []
    for b in range(NB):
        keys = TB * (b + 1)
        s = st[:keys, b * D : (b + 1) * D]
        key = lax.broadcasted_iota(jnp.int32, (keys, D), 0)
        tok = TB * b + lax.broadcasted_iota(jnp.int32, (keys, D), 1) // QH
        s = jnp.where(key <= tok, s, -1e30)
        top = jnp.max(s, axis=0, keepdims=True)
        p = jnp.exp2((s - top) * SCALE2)
        inv = 1.0 / jnp.sum(p, axis=0, keepdims=True)
        inv = jnp.where(tok[:1] < length, inv, 0.0)
        w = (p * inv).astype(BF16)
        w = jnp.dot(w, perm, preferred_element_type=F32).astype(BF16)
        out.append(w)
    return out


def main_kernel(
    sq, spair, lq, lpair, tabs,
    recv_out, long_out,
    gq, gkv, pbuf, skv, lkv, kscr, vscr, kslot, send, lall, lqv, lout, acc, mx, sm, otile,
    xq_send, xq_recv, xk_send, xk_recv, z_send, z_recv, v_send, v_recv,
    l_send, l_recv, f_send, f_recv, loc_sem,
):
    g = lax.axis_index("grp")
    h = lax.axis_index("head")
    y, z = g // 8, g % 8
    x, core = h // 2, h % 2

    def group_at(i):
        m = i % 8
        oz = jnp.where(m % 2 == 0, m // 2 + 1, 8 - (m // 2 + 1))
        oz = jnp.where(m == 7, 0, oz)
        oy = i // 8
        return ((y + oy) % 4) * 8 + (z + oz) % 8, ((y + 4 - oy) % 4) * 8 + (z + 8 - oz) % 8

    SELF = 7

    barrier = pltpu.get_barrier_semaphore()

    @pl.loop(1, NG)
    def _(o):
        pl.semaphore_signal(barrier, inc=1, device_id=((g + o) % NG, h), device_id_type=MESH)

    for o in range(1, NH):
        pl.semaphore_signal(barrier, inc=1, device_id=(g, (h + o) % NH), device_id_type=MESH)

    own = pl.ds(pl.multiple_of(h * TOK, TOK), TOK)
    own_kv = pl.ds(h * (TOK // TB), TOK // TB)
    in_sp = pltpu.make_async_copy(spair, pbuf.at[0], loc_sem.at[0])
    in_lp = pltpu.make_async_copy(lpair, pbuf.at[1], loc_sem.at[1])
    in_lq = pltpu.make_async_copy(lq, lqv, loc_sem.at[2])
    own_q = pltpu.make_async_copy(sq.at[:, h], gq.at[own], loc_sem.at[3])
    in_sp.start()
    in_lp.start()
    in_lq.start()
    own_q.start()

    def by_head(n, store):
        for t in range(TOK // 32):
            part = pbuf[n, t * 32 : (t + 1) * 32].astype(F32).reshape(32 * NH, 2 * D)
            kscr[t * 32 * NH : (t + 1) * 32 * NH, :] = part[:, :D]
            vscr[t * 32 * NH : (t + 1) * 32 * NH, :] = part[:, D:]
        for c in range(NH):
            store(c, kscr[pl.ds(c, TOK, stride=NH), :].astype(BF16), vscr[pl.ds(c, TOK, stride=NH), :].astype(BF16))

    def store_short(c, k, v):
        skv[c, :, :, :D] = k.reshape(TOK // TB, TB, D)
        skv[c, :, :, D:] = v.reshape(TOK // TB, TB, D)

    def store_long(c, k, v):
        lkv[c, :, :D] = k
        lkv[c, :, D:] = v

    in_sp.wait()
    by_head(0, store_short)
    gq[NH * TOK :, :, :] = jnp.zeros((DOC, QH, D), BF16)
    gkv[NH * TOK // TB :] = jnp.zeros((KROWS // TB, TB, 2 * D), BF16)
    pl.semaphore_wait(barrier, NH - 1 + NG - 1)

    def k_copy(o):
        peer = (h + o) % NH
        return pltpu.make_async_remote_copy(
            skv.at[peer], gkv.at[own_kv], xk_send.at[o], xk_recv.at[o],
            device_id=(g, peer), device_id_type=MESH)

    def q_copy(o):
        peer = (h + o) % NH
        return pltpu.make_async_remote_copy(
            sq.at[:, peer], gq.at[own], xq_send.at[o], xq_recv.at[o],
            device_id=(g, peer), device_id_type=MESH)

    for o in range(1, NH):
        k_copy(o).start()
    for o in range(1, NH):
        q_copy(o).start()
    own_k = pltpu.make_async_copy(skv.at[h], gkv.at[own_kv], loc_sem.at[4])
    own_k.start()

    partner = h + 1 - 2 * core

    def l_copy(n):
        return pltpu.make_async_remote_copy(
            lkv, lall.at[h], l_send.at[n], l_recv.at[n],
            device_id=(g, (h + 2 * n) % NH), device_id_type=MESH)

    def f_copy(n):
        src = (h + NH - 2 * n) % NH
        return pltpu.make_async_remote_copy(
            lall.at[src], lall.at[src], f_send.at[n], f_recv.at[n],
            device_id=(g, partner), device_id_type=MESH)

    l_pair = pltpu.make_async_remote_copy(
        lkv, lall.at[h], f_send.at[0], f_recv.at[0],
        device_id=(g, partner), device_id_type=MESH)
    own_l = pltpu.make_async_copy(lkv, lall.at[h], loc_sem.at[5])

    in_lp.wait()
    by_head(1, store_long)
    l_pair.start()
    own_l.start()

    def v_copy(i):
        to, _ = group_at(i)
        return pltpu.make_async_remote_copy(
            send.at[i, pl.ds(WROWS, DOC)], recv_out.at[g, pl.ds(WROWS, DOC)], v_send.at[i], v_recv.at[i],
            device_id=(to, h), device_id_type=MESH)

    def z_copy(i):
        to, _ = group_at(i)
        return pltpu.make_async_remote_copy(
            send.at[i, pl.ds(0, WROWS)], recv_out.at[g, pl.ds(0, WROWS)], z_send.at[i], z_recv.at[i],
            device_id=(to, h), device_id_type=MESH)

    def slot_pair(i):
        to, _ = group_at(i)
        kv = gkv[pl.ds(tabs[2, to], KROWS // TB)].reshape(KROWS, 2 * D)
        pick = lax.broadcasted_iota(jnp.int32, (DOC, KROWS), 0) + tabs[3, to]
        pick = (pick == lax.broadcasted_iota(jnp.int32, (DOC, KROWS), 1)).astype(BF16)
        kv = jnp.dot(pick, kv, preferred_element_type=F32).astype(BF16)
        kslot[i] = kv[:, :D]
        send[i, WROWS:SLOT, :] = kv[:, D:]

    perm = perm_matrix()

    def slot(i):
        to, _ = group_at(i)
        q = gq[pl.ds(tabs[0, to], DOC)].astype(F32).reshape(DOC * QH, D).astype(BF16)
        for b, w in enumerate(slot_weights(q, kslot[i], tabs[1, to], perm)):
            send[i, wrow(b) : wrow(b + 1), :] = w

    own_slot = pltpu.make_async_copy(send.at[SELF], recv_out.at[g], loc_sem.at[6])

    GROUP = 4

    def in_groups(work, copy):
        def start(j):
            for d in range(GROUP):
                i = j * GROUP + d

                @pl.when(i != SELF)
                def _(i=i):
                    copy(i).start()

        def step(j):
            for d in range(GROUP):
                work(j * GROUP + d)

        step(0)

        @pl.loop(1, NG // GROUP)
        def _(j):
            step(j)
            start(j - 1)

        start(jnp.int32(NG // GROUP - 1))

    own_k.wait()
    for o in range(1, NH):
        k_copy(o).wait_recv()
    in_groups(slot_pair, v_copy)

    R = 32
    M = R * QH
    TILES = NH * TOK // R

    def long_block(n, first):
        at = 2 * (x - n)

        def tile(i, _):
            c, t = i // (TOK // R), i % (TOK // R)
            rows = pl.ds(pl.multiple_of(i * M, M), M)
            q = lqv[pl.ds(t * R, R), c].astype(F32).reshape(M, D).astype(BF16)
            k = lall[pl.ds(at, 2), c, :, 0:D].reshape(2 * TOK, D)
            v = lall[pl.ds(at, 2), c, :, D : 2 * D].reshape(2 * TOK, D)
            s = lax.dot_general(q, k, (((1,), (1,)), ((), ())), preferred_element_type=F32)
            if first:
                row = core * TOK + t * R + lax.broadcasted_iota(jnp.int32, (M, 2 * TOK), 0) // QH
                col = lax.broadcasted_iota(jnp.int32, (M, 2 * TOK), 1)
                s = jnp.where(col <= row, s, -1e30)
            top = jnp.max(jnp.maximum(s[:, :D], s[:, D:]), axis=1, keepdims=True)
            top = jnp.broadcast_to(top, (M, D))
            if not first:
                old = mx[rows, :]
                top = jnp.maximum(old, top)
                fade = jnp.exp2((old - top) * SCALE2)
            p0 = jnp.exp2((s[:, :D] - top) * SCALE2)
            p1 = jnp.exp2((s[:, D:] - top) * SCALE2)
            p = jnp.concatenate([p0.astype(BF16), p1.astype(BF16)], axis=1)
            part = jnp.dot(p, v, preferred_element_type=F32)
            mx[rows, :] = top
            if first:
                sm[rows, :] = p0 + p1
                acc[rows, :] = part
            else:
                sm[rows, :] = sm[rows, :] * fade + (p0 + p1)
                acc[rows, :] = acc[rows, :] * fade + part
            return 0

        lax.fori_loop(0, TILES, tile, 0, unroll=8)

    in_lq.wait()
    own_l.wait()
    l_pair.wait_recv()
    long_block(0, True)

    own_q.wait()
    for o in range(1, NH):
        q_copy(o).wait_recv()
    for o in range(1, NH):
        k_copy(o).wait_send()
        q_copy(o).wait_send()
    for n in range(1, 4):
        @pl.when(x + n < 4)
        def _(n=n):
            l_copy(n).start()

    in_groups(slot, z_copy)
    own_slot.start()

    for n in range(1, 4):
        @pl.when(x >= n)
        def _(n=n):
            l_copy(n).wait_recv()
            f_copy(n).start()

    @pl.loop(1, x + 1)
    def _(n):
        f_copy(n).wait_recv()
        long_block(n, False)

    def out_copy(c):
        return pltpu.make_async_copy(
            lout.at[c], long_out.at[:, pl.ds(pl.multiple_of(c * QH * D, QH * D), QH * D)], loc_sem.at[8 + c])

    @pl.loop(0, NH)
    def _(c):
        for t in range(TOK // R):
            rows = pl.ds(pl.multiple_of((c * (TOK // R) + t) * M, M), M)
            total = jnp.sum(sm[rows, :], axis=1, keepdims=True)
            otile[t * M : (t + 1) * M, :] = acc[rows, :] * (1.0 / total)
        for t in range(TOK // R):
            for e in range(QH):
                part = otile[pl.ds(t * M + e, R, stride=QH), :].astype(BF16)
                lout[c, t * R : (t + 1) * R, e * D : (e + 1) * D] = part
        out_copy(c).start()

    l_pair.wait_send()
    for n in range(1, 4):
        @pl.when(x + n < 4)
        def _(n=n):
            l_copy(n).wait_send()

        @pl.when(x >= n)
        def _(n=n):
            f_copy(n).wait_send()

    @pl.loop(0, NG)
    def _(i):
        @pl.when(i != SELF)
        def _():
            _, source = group_at(i)
            for lo, size, ss, rs in ((WROWS, DOC, v_send, v_recv), (0, WROWS, z_send, z_recv)):
                pltpu.make_async_remote_copy(
                    send.at[i, pl.ds(lo, size)], recv_out.at[source, pl.ds(lo, size)], ss.at[i], rs.at[i],
                    device_id=(source, h), device_id_type=MESH).wait()

    own_slot.wait()
    for c in range(NH):
        out_copy(c).wait()


def exchange(sq, spair, lq, lpair, tabs):
    any_spec = pl.BlockSpec(memory_space=pl.ANY)
    smem = pl.BlockSpec(memory_space=pltpu.SMEM)
    dma = pltpu.SemaphoreType.DMA
    return pl.pallas_call(
        main_kernel,
        out_shape=(
            jax.ShapeDtypeStruct((NG, SLOT, D), BF16),
            jax.ShapeDtypeStruct((TOK, NH * QH * D), BF16),
        ),
        in_specs=[any_spec] * 4 + [smem],
        out_specs=(any_spec, any_spec),
        scratch_shapes=[
            pltpu.VMEM((NH * TOK + DOC, QH, D), BF16),
            pltpu.VMEM(((NH * TOK + KROWS) // TB, TB, 2 * D), BF16),
            pltpu.VMEM((2, TOK, NH, 2 * D), BF16),
            pltpu.VMEM((NH, TOK // TB, TB, 2 * D), BF16),
            pltpu.VMEM((NH, TOK, 2 * D), BF16),
            pltpu.VMEM((TOK * NH, D), F32),
            pltpu.VMEM((TOK * NH, D), F32),
            pltpu.VMEM((NG, DOC, D), BF16),
            pltpu.VMEM((NG, SLOT, D), BF16),
            pltpu.VMEM((NH, NH, TOK, 2 * D), BF16),
            pltpu.VMEM((TOK, NH, QH, D), BF16),
            pltpu.VMEM((NH, TOK, QH * D), BF16),
            pltpu.VMEM((TOK * NH * QH, D), F32),
            pltpu.VMEM((TOK * NH * QH, D), F32),
            pltpu.VMEM((TOK * NH * QH, D), F32),
            pltpu.VMEM((TOK * QH, D), F32),
            dma((NH,)), dma((NH,)), dma((NH,)), dma((NH,)),
            dma((NG,)), dma((NG,)), dma((NG,)), dma((NG,)),
            dma((4,)), dma((4,)), dma((4,)), dma((4,)),
            dma((16,)),
        ],
        compiler_params=pltpu.CompilerParams(collective_id=0, has_side_effects=True),
        name="exchange",
    )(sq, spair, lq, lpair, tabs)


def place_kernel(per_step, got, long_in, short_out, long_out):
    long_out[...] = long_in[...]
    for s in range(per_step):
        v = got[s, WROWS:SLOT, :]
        for b in range(NB):
            w = got[s, wrow(b) : wrow(b + 1), :]
            o = lax.dot_general(w, v[: TB * (b + 1)], (((0,), (0,)), ((), ())), preferred_element_type=F32)
            o = o.astype(BF16)
            at = s * DOC + b * TB
            for e in range(QH):
                short_out[at : at + TB, e * D : (e + 1) * D] = o[e * TB : (e + 1) * TB, :]


def place(got, long_in):
    per_step = 4
    steps = NG // per_step
    return pl.pallas_call(
        functools.partial(place_kernel, per_step),
        grid=(steps,),
        out_shape=(
            jax.ShapeDtypeStruct((NG * DOC, QH * D), BF16),
            jax.ShapeDtypeStruct((TOK, NH * QH * D), BF16),
        ),
        in_specs=[
            pl.BlockSpec((per_step, SLOT, D), lambda i: (i, 0, 0)),
            pl.BlockSpec((TOK // steps, NH * QH * D), lambda i: (i, 0)),
        ],
        out_specs=(
            pl.BlockSpec((per_step * DOC, QH * D), lambda i: (i, 0)),
            pl.BlockSpec((TOK // steps, NH * QH * D), lambda i: (i, 0)),
        ),
        name="place",
    )(got, long_in)


def slot_tables(doc_lengths, destinations):
    g = lax.axis_index("grp")
    lens = lax.dynamic_index_in_dim(doc_lengths, g, 0, keepdims=False)
    dest = lax.dynamic_index_in_dim(destinations, g, 0, keepdims=False)
    doc = jnp.arange(NG, dtype=jnp.int32)
    hit = dest[None, :] == doc[:, None]
    before = jnp.where(doc[None, :] < doc[:, None], lens[None, :], 0).sum(axis=1)
    start = jnp.where(hit, before[None, :], 0).sum(axis=1)
    rows = jnp.where(hit, lens[None, :], 0).sum(axis=1)
    return jnp.stack([start, rows, start // TB, start % TB])


def on_device(long_queries, long_pairs, short_queries, short_pairs, doc_lengths, destinations):
    split = (TOK, NH, QH, D)
    got, long_mix = exchange(
        short_queries.reshape(split),
        short_pairs,
        long_queries.reshape(split),
        long_pairs,
        slot_tables(doc_lengths, destinations),
    )
    short_placed, long_result = place(got, long_mix)
    return long_result, short_placed


def solution(mesh):
    rows = P(("grp", "head"), None, None)
    return jax.shard_map(
        on_device,
        mesh=mesh,
        in_specs=(rows, rows, rows, rows, P(), P()),
        out_specs=(P(("grp", "head"), None), P("grp", "head")),
        check_vma=False,
    )
```

```python
import functools
import math

import jax
import jax.numpy as jnp
from jax import lax
from jax.experimental import pallas as pl
from jax.experimental.pallas import tpu as pltpu
from jax.sharding import PartitionSpec as P

MESH = pl.DeviceIdType.MESH
BF16 = jnp.bfloat16
F32 = jnp.float32

NG = 32
NH = 8
TOK = 128
QH = 8
D = 128
DOC = 64
TB = 16
NB = DOC // TB
WROWS = TB * NB * (NB + 1) // 2
SLOT = WROWS + DOC
KROWS = DOC + TB
SCALE2 = math.log2(math.e) / math.sqrt(D)


def wrow(block):
    return TB * block * (block + 1) // 2


def perm_matrix():
    row = lax.broadcasted_iota(jnp.int32, (D, D), 0)
    col = lax.broadcasted_iota(jnp.int32, (D, D), 1)
    return (col == (row % QH) * TB + row // QH).astype(BF16)


def slot_weights(q, k, length, perm):
    st = lax.dot_general(k, q, (((1,), (1,)), ((), ())), preferred_element_type=F32)
    out = []
    for b in range(NB):
        keys = TB * (b + 1)
        s = st[:keys, b * D : (b + 1) * D]
        key = lax.broadcasted_iota(jnp.int32, (keys, D), 0)
        tok = TB * b + lax.broadcasted_iota(jnp.int32, (keys, D), 1) // QH
        s = jnp.where(key <= tok, s, -1e30)
        top = jnp.max(s, axis=0, keepdims=True)
        p = jnp.exp2((s - top) * SCALE2)
        inv = 1.0 / jnp.sum(p, axis=0, keepdims=True)
        inv = jnp.where(tok[:1] < length, inv, 0.0)
        w = (p * inv).astype(BF16)
        w = jnp.dot(w, perm, preferred_element_type=F32).astype(BF16)
        out.append(w)
    return out


def main_kernel(
    sq, spair, lq, lpair, tabs,
    recv_out, long_out,
    gq, gkv, pbuf, skv, lkv, kscr, vscr, kslot, send, lall, lqv, lout, acc, mx, sm, otile,
    xq_send, xq_recv, xk_send, xk_recv, z_send, z_recv, v_send, v_recv,
    l_send, l_recv, f_send, f_recv, loc_sem,
):
    g = lax.axis_index("grp")
    h = lax.axis_index("head")
    y, z = g // 8, g % 8
    x, core = h // 2, h % 2

    def group_at(i):
        m = i % 8
        oz = jnp.where(m % 2 == 0, m // 2 + 1, 8 - (m // 2 + 1))
        oz = jnp.where(m == 7, 0, oz)
        oy = i // 8
        return ((y + oy) % 4) * 8 + (z + oz) % 8, ((y + 4 - oy) % 4) * 8 + (z + 8 - oz) % 8

    SELF = 7

    barrier = pltpu.get_barrier_semaphore()

    @pl.loop(1, NG)
    def _(o):
        pl.semaphore_signal(barrier, inc=1, device_id=((g + o) % NG, h), device_id_type=MESH)

    for o in range(1, NH):
        pl.semaphore_signal(barrier, inc=1, device_id=(g, (h + o) % NH), device_id_type=MESH)

    own = pl.ds(pl.multiple_of(h * TOK, TOK), TOK)
    own_kv = pl.ds(h * (TOK // TB), TOK // TB)
    in_sp = pltpu.make_async_copy(spair, pbuf.at[0], loc_sem.at[0])
    in_lp = pltpu.make_async_copy(lpair, pbuf.at[1], loc_sem.at[1])
    in_lq = pltpu.make_async_copy(lq, lqv, loc_sem.at[2])
    own_q = pltpu.make_async_copy(sq.at[:, h], gq.at[own], loc_sem.at[3])
    in_sp.start()
    in_lp.start()
    in_lq.start()
    own_q.start()

    def by_head(n, store):
        for t in range(TOK // 32):
            part = pbuf[n, t].astype(F32).reshape(32 * NH, 2 * D)
            kscr[t * 32 * NH : (t + 1) * 32 * NH, :] = part[:, :D]
            vscr[t * 32 * NH : (t + 1) * 32 * NH, :] = part[:, D:]
        for c in range(NH):
            store(c, kscr[pl.ds(c, TOK, stride=NH), :].astype(BF16), vscr[pl.ds(c, TOK, stride=NH), :].astype(BF16))

    def store_short(c, k, v):
        skv[c, :, :, :D] = k.reshape(TOK // TB, TB, D)
        skv[c, :, :, D:] = v.reshape(TOK // TB, TB, D)

    def store_long(c, k, v):
        lkv[c, :, :D] = k
        lkv[c, :, D:] = v

    in_sp.wait()
    by_head(0, store_short)
    gq[NH * TOK :, :, :] = jnp.zeros((DOC, QH, D), BF16)
    gkv[NH * TOK // TB :] = jnp.zeros((KROWS // TB, TB, 2 * D), BF16)
    pl.semaphore_wait(barrier, NH - 1 + NG - 1)

    def k_copy(o):
        peer = (h + o) % NH
        return pltpu.make_async_remote_copy(
            skv.at[peer], gkv.at[own_kv], xk_send.at[o], xk_recv.at[o],
            device_id=(g, peer), device_id_type=MESH)

    def q_copy(o):
        peer = (h + o) % NH
        return pltpu.make_async_remote_copy(
            sq.at[:, peer], gq.at[own], xq_send.at[o], xq_recv.at[o],
            device_id=(g, peer), device_id_type=MESH)

    for o in range(1, NH):
        k_copy(o).start()
    for o in range(1, NH):
        q_copy(o).start()
    own_k = pltpu.make_async_copy(skv.at[h], gkv.at[own_kv], loc_sem.at[4])
    own_k.start()

    partner = h + 1 - 2 * core

    def l_copy(n):
        return pltpu.make_async_remote_copy(
            lkv, lall.at[h], l_send.at[n], l_recv.at[n],
            device_id=(g, (h + 2 * n) % NH), device_id_type=MESH)

    def f_copy(n):
        src = (h + NH - 2 * n) % NH
        return pltpu.make_async_remote_copy(
            lall.at[src], lall.at[src], f_send.at[n], f_recv.at[n],
            device_id=(g, partner), device_id_type=MESH)

    l_pair = pltpu.make_async_remote_copy(
        lkv, lall.at[h], f_send.at[0], f_recv.at[0],
        device_id=(g, partner), device_id_type=MESH)
    own_l = pltpu.make_async_copy(lkv, lall.at[h], loc_sem.at[5])

    in_lp.wait()
    by_head(1, store_long)
    l_pair.start()
    own_l.start()

    def v_copy(i):
        to, _ = group_at(i)
        return pltpu.make_async_remote_copy(
            send.at[i, pl.ds(WROWS, DOC)], recv_out.at[g, pl.ds(WROWS, DOC)], v_send.at[i], v_recv.at[i],
            device_id=(to, h), device_id_type=MESH)

    def z_copy(i):
        to, _ = group_at(i)
        return pltpu.make_async_remote_copy(
            send.at[i, pl.ds(0, WROWS)], recv_out.at[g, pl.ds(0, WROWS)], z_send.at[i], z_recv.at[i],
            device_id=(to, h), device_id_type=MESH)

    def slot_pair(i):
        to, _ = group_at(i)
        kv = gkv[pl.ds(tabs[2, to], KROWS // TB)].reshape(KROWS, 2 * D)
        pick = lax.broadcasted_iota(jnp.int32, (DOC, KROWS), 0) + tabs[3, to]
        pick = (pick == lax.broadcasted_iota(jnp.int32, (DOC, KROWS), 1)).astype(BF16)
        kv = jnp.dot(pick, kv, preferred_element_type=F32).astype(BF16)
        kslot[i] = kv[:, :D]
        send[i, WROWS:SLOT, :] = kv[:, D:]

    perm = perm_matrix()

    def slot(i):
        to, _ = group_at(i)
        q = gq[pl.ds(tabs[0, to], DOC)].astype(F32).reshape(DOC * QH, D).astype(BF16)
        for b, w in enumerate(slot_weights(q, kslot[i], tabs[1, to], perm)):
            send[i, wrow(b) : wrow(b + 1), :] = w

    own_slot = pltpu.make_async_copy(send.at[SELF], recv_out.at[g], loc_sem.at[6])

    GROUP = 4

    def in_groups(work, copy):
        def start(j):
            for d in range(GROUP):
                i = j * GROUP + d

                @pl.when(i != SELF)
                def _(i=i):
                    copy(i).start()

        def step(j):
            for d in range(GROUP):
                work(j * GROUP + d)

        step(0)

        @pl.loop(1, NG // GROUP)
        def _(j):
            step(j)
            start(j - 1)

        start(jnp.int32(NG // GROUP - 1))

    own_k.wait()
    for o in range(1, NH):
        k_copy(o).wait_recv()
    in_groups(slot_pair, v_copy)

    R = 32
    M = R * QH
    TILES = NH * TOK // R

    def long_block(n, first):
        at = 2 * (x - n)

        def tile(i, _):
            c, t = i // (TOK // R), i % (TOK // R)
            rows = pl.ds(pl.multiple_of(i * M, M), M)
            q = lqv[pl.ds(t * R, R), c].astype(F32).reshape(M, D).astype(BF16)
            k = lall[pl.ds(at, 2), c, :, 0:D].reshape(2 * TOK, D)
            v = lall[pl.ds(at, 2), c, :, D : 2 * D].reshape(2 * TOK, D)
            s = lax.dot_general(q, k, (((1,), (1,)), ((), ())), preferred_element_type=F32)
            if first:
                row = core * TOK + t * R + lax.broadcasted_iota(jnp.int32, (M, 2 * TOK), 0) // QH
                col = lax.broadcasted_iota(jnp.int32, (M, 2 * TOK), 1)
                s = jnp.where(col <= row, s, -1e30)
            top = jnp.max(jnp.maximum(s[:, :D], s[:, D:]), axis=1, keepdims=True)
            top = jnp.broadcast_to(top, (M, D))
            if not first:
                old = mx[rows, :]
                top = jnp.maximum(old, top)
                fade = jnp.exp2((old - top) * SCALE2)
            p0 = jnp.exp2((s[:, :D] - top) * SCALE2)
            p1 = jnp.exp2((s[:, D:] - top) * SCALE2)
            p = jnp.concatenate([p0.astype(BF16), p1.astype(BF16)], axis=1)
            part = jnp.dot(p, v, preferred_element_type=F32)
            mx[rows, :] = top
            if first:
                sm[rows, :] = p0 + p1
                acc[rows, :] = part
            else:
                sm[rows, :] = sm[rows, :] * fade + (p0 + p1)
                acc[rows, :] = acc[rows, :] * fade + part
            return 0

        lax.fori_loop(0, TILES, tile, 0, unroll=8)

    in_lq.wait()
    own_l.wait()
    l_pair.wait_recv()
    long_block(0, True)

    own_q.wait()
    for o in range(1, NH):
        q_copy(o).wait_recv()
    for o in range(1, NH):
        k_copy(o).wait_send()
        q_copy(o).wait_send()
    for n in range(1, 4):
        @pl.when(x + n < 4)
        def _(n=n):
            l_copy(n).start()

    in_groups(slot, z_copy)
    own_slot.start()

    @pl.loop(1, x + 1)
    def _(n):
        l_copy(n).wait_recv()
        f_copy(n).start()
        f_copy(n).wait_recv()
        long_block(n, False)

    def out_copy(c):
        return pltpu.make_async_copy(
            lout.at[c], long_out.at[:, pl.ds(pl.multiple_of(c * QH * D, QH * D), QH * D)], loc_sem.at[8 + c])

    @pl.loop(0, NH)
    def _(c):
        for t in range(TOK // R):
            rows = pl.ds(pl.multiple_of((c * (TOK // R) + t) * M, M), M)
            total = jnp.sum(sm[rows, :], axis=1, keepdims=True)
            otile[t * M : (t + 1) * M, :] = acc[rows, :] * (1.0 / total)
        for t in range(TOK // R):
            for e in range(QH):
                part = otile[pl.ds(t * M + e, R, stride=QH), :].astype(BF16)
                lout[c, t * R : (t + 1) * R, e * D : (e + 1) * D] = part
        out_copy(c).start()

    l_pair.wait_send()
    for n in range(1, 4):
        @pl.when(x + n < 4)
        def _(n=n):
            l_copy(n).wait_send()

        @pl.when(x >= n)
        def _(n=n):
            f_copy(n).wait_send()

    @pl.loop(0, NG)
    def _(i):
        @pl.when(i != SELF)
        def _():
            _, source = group_at(i)
            for lo, size, ss, rs in ((WROWS, DOC, v_send, v_recv), (0, WROWS, z_send, z_recv)):
                pltpu.make_async_remote_copy(
                    send.at[i, pl.ds(lo, size)], recv_out.at[source, pl.ds(lo, size)], ss.at[i], rs.at[i],
                    device_id=(source, h), device_id_type=MESH).wait()

    own_slot.wait()
    for c in range(NH):
        out_copy(c).wait()


def exchange(sq, spair, lq, lpair, tabs):
    any_spec = pl.BlockSpec(memory_space=pl.ANY)
    smem = pl.BlockSpec(memory_space=pltpu.SMEM)
    dma = pltpu.SemaphoreType.DMA
    return pl.pallas_call(
        main_kernel,
        out_shape=(
            jax.ShapeDtypeStruct((NG, SLOT, D), BF16),
            jax.ShapeDtypeStruct((TOK, NH * QH * D), BF16),
        ),
        in_specs=[any_spec] * 4 + [smem],
        out_specs=(any_spec, any_spec),
        scratch_shapes=[
            pltpu.VMEM((NH * TOK + DOC, QH, D), BF16),
            pltpu.VMEM(((NH * TOK + KROWS) // TB, TB, 2 * D), BF16),
            pltpu.VMEM((2, TOK // 32, 32, NH, 2 * D), BF16),
            pltpu.VMEM((NH, TOK // TB, TB, 2 * D), BF16),
            pltpu.VMEM((NH, TOK, 2 * D), BF16),
            pltpu.VMEM((TOK * NH, D), F32),
            pltpu.VMEM((TOK * NH, D), F32),
            pltpu.VMEM((NG, DOC, D), BF16),
            pltpu.VMEM((NG, SLOT, D), BF16),
            pltpu.VMEM((NH, NH, TOK, 2 * D), BF16),
            pltpu.VMEM((TOK, NH, QH, D), BF16),
            pltpu.VMEM((NH, TOK, QH * D), BF16),
            pltpu.VMEM((TOK * NH * QH, D), F32),
            pltpu.VMEM((TOK * NH * QH, D), F32),
            pltpu.VMEM((TOK * NH * QH, D), F32),
            pltpu.VMEM((TOK * QH, D), F32),
            dma((NH,)), dma((NH,)), dma((NH,)), dma((NH,)),
            dma((NG,)), dma((NG,)), dma((NG,)), dma((NG,)),
            dma((4,)), dma((4,)), dma((4,)), dma((4,)),
            dma((16,)),
        ],
        compiler_params=pltpu.CompilerParams(
            collective_id=0, has_side_effects=True, vmem_limit_bytes=48 << 20),
        name="exchange",
    )(sq, spair, lq, lpair, tabs)


def place_kernel(got, long_in, short_out, long_out, gbuf, obuf, lbuf, in_sem, out_sem, l_sem):
    per_step = 4
    steps = NG // per_step

    def g_copy(j):
        part = pl.ds(j * per_step, per_step)
        return pltpu.make_async_copy(got.at[part], gbuf.at[part], in_sem.at[j])

    def o_copy(j):
        part = pl.ds(pl.multiple_of(j * per_step * DOC, per_step * DOC), per_step * DOC)
        return pltpu.make_async_copy(obuf.at[part], short_out.at[part], out_sem.at[j])

    l_get = pltpu.make_async_copy(long_in, lbuf, l_sem.at[0])
    l_put = pltpu.make_async_copy(lbuf, long_out, l_sem.at[1])
    for j in range(steps):
        g_copy(j).start()
    l_get.start()

    def step(j, _):
        g_copy(j).wait()
        for d in range(per_step):
            s = j * per_step + d
            v = gbuf[s, WROWS:SLOT, :]
            for b in range(NB):
                w = gbuf[s, wrow(b) : wrow(b + 1), :]
                o = lax.dot_general(w, v[: TB * (b + 1)], (((0,), (0,)), ((), ())), preferred_element_type=F32)
                o = o.astype(BF16)
                rows = pl.ds(pl.multiple_of(s * DOC + b * TB, TB), TB)
                for e in range(QH):
                    obuf[rows, e * D : (e + 1) * D] = o[e * TB : (e + 1) * TB, :]
        o_copy(j).start()
        return 0

    step(0, 0)
    l_get.wait()
    l_put.start()
    lax.fori_loop(1, steps, step, 0)
    for j in range(steps):
        o_copy(j).wait()
    l_put.wait()


def place(got, long_in):
    any_spec = pl.BlockSpec(memory_space=pl.ANY)
    dma = pltpu.SemaphoreType.DMA
    return pl.pallas_call(
        place_kernel,
        out_shape=(
            jax.ShapeDtypeStruct((NG * DOC, QH * D), BF16),
            jax.ShapeDtypeStruct((TOK, NH * QH * D), BF16),
        ),
        in_specs=[any_spec, any_spec],
        out_specs=(any_spec, any_spec),
        scratch_shapes=[
            pltpu.VMEM((NG, SLOT, D), BF16),
            pltpu.VMEM((NG * DOC, QH * D), BF16),
            pltpu.VMEM((TOK, NH * QH * D), BF16),
            dma((8,)), dma((8,)), dma((2,)),
        ],
        compiler_params=pltpu.CompilerParams(vmem_limit_bytes=24 << 20),
        name="place",
    )(got, long_in)


def slot_tables(doc_lengths, destinations):
    g = lax.axis_index("grp")
    lens = lax.dynamic_index_in_dim(doc_lengths, g, 0, keepdims=False)
    dest = lax.dynamic_index_in_dim(destinations, g, 0, keepdims=False)
    doc = jnp.arange(NG, dtype=jnp.int32)
    hit = dest[None, :] == doc[:, None]
    before = jnp.where(doc[None, :] < doc[:, None], lens[None, :], 0).sum(axis=1)
    start = jnp.where(hit, before[None, :], 0).sum(axis=1)
    rows = jnp.where(hit, lens[None, :], 0).sum(axis=1)
    return jnp.stack([start, rows, start // TB, start % TB])


def on_device(long_queries, long_pairs, short_queries, short_pairs, doc_lengths, destinations):
    queries = (TOK, NH, QH, D)
    pairs = (TOK // 32, 32, NH, 2 * D)

    def stay(array, shape):
        return pltpu.with_memory_space_constraint(array.reshape(shape), pltpu.HBM)

    got, long_mix = exchange(
        stay(short_queries, queries),
        stay(short_pairs, pairs),
        stay(long_queries, queries),
        stay(long_pairs, pairs),
        slot_tables(doc_lengths, destinations),
    )
    short_placed, long_result = place(got, long_mix)
    return long_result, short_placed


def solution(mesh):
    rows = P(("grp", "head"), None, None)
    return jax.shard_map(
        on_device,
        mesh=mesh,
        in_specs=(rows, rows, rows, rows, P(), P()),
        out_specs=(P(("grp", "head"), None), P("grp", "head")),
        check_vma=False,
    )
```

```python
import functools
import math

import jax
import jax.numpy as jnp
from jax import lax
from jax.experimental import pallas as pl
from jax.experimental.pallas import tpu as pltpu
from jax.sharding import PartitionSpec as P

MESH = pl.DeviceIdType.MESH
BF16 = jnp.bfloat16
F32 = jnp.float32

NG = 32
NH = 8
TOK = 128
QH = 8
D = 128
DOC = 64
TB = 16
NB = DOC // TB
WROWS = TB * NB * (NB + 1) // 2
SLOT = WROWS + DOC
KROWS = DOC + TB
SCALE2 = math.log2(math.e) / math.sqrt(D)


def wrow(block):
    return TB * block * (block + 1) // 2


def perm_matrix():
    row = lax.broadcasted_iota(jnp.int32, (D, D), 0)
    col = lax.broadcasted_iota(jnp.int32, (D, D), 1)
    return (col == (row % QH) * TB + row // QH).astype(BF16)


def slot_weights(q, k, length, perm):
    st = lax.dot_general(k, q, (((1,), (1,)), ((), ())), preferred_element_type=F32)
    out = []
    for b in range(NB):
        keys = TB * (b + 1)
        s = st[:keys, b * D : (b + 1) * D]
        key = lax.broadcasted_iota(jnp.int32, (keys, D), 0)
        tok = TB * b + lax.broadcasted_iota(jnp.int32, (keys, D), 1) // QH
        s = jnp.where(key <= tok, s, -1e30)
        top = jnp.max(s, axis=0, keepdims=True)
        p = jnp.exp2((s - top) * SCALE2)
        inv = 1.0 / jnp.sum(p, axis=0, keepdims=True)
        inv = jnp.where(tok[:1] < length, inv, 0.0)
        w = (p * inv).astype(BF16)
        w = jnp.dot(w, perm, preferred_element_type=F32).astype(BF16)
        out.append(w)
    return out


def main_kernel(
    sq, spair, lq, lpair, tabs,
    recv_out, long_out,
    gq, gkv, pbuf, skv, lkv, kscr, vscr, kslot, send, lall, lqv, lout, acc, mx, sm, otile,
    xq_send, xq_recv, xk_send, xk_recv, z_send, z_recv, v_send, v_recv,
    l_send, l_recv, f_send, f_recv, loc_sem,
):
    g = lax.axis_index("grp")
    h = lax.axis_index("head")
    y, z = g // 8, g % 8
    x, core = h // 2, h % 2

    def group_at(i):
        m = i % 8
        oz = jnp.where(m % 2 == 0, m // 2 + 1, 8 - (m // 2 + 1))
        oz = jnp.where(m == 7, 0, oz)
        oy = i // 8
        return ((y + oy) % 4) * 8 + (z + oz) % 8, ((y + 4 - oy) % 4) * 8 + (z + 8 - oz) % 8

    SELF = 7

    barrier = pltpu.get_barrier_semaphore()

    @pl.loop(1, NG)
    def _(o):
        pl.semaphore_signal(barrier, inc=1, device_id=((g + o) % NG, h), device_id_type=MESH)

    for o in range(1, NH):
        pl.semaphore_signal(barrier, inc=1, device_id=(g, (h + o) % NH), device_id_type=MESH)

    own = pl.ds(pl.multiple_of(h * TOK, TOK), TOK)
    own_kv = pl.ds(h * (TOK // TB), TOK // TB)
    in_sp = pltpu.make_async_copy(spair, pbuf.at[0], loc_sem.at[0])
    in_lp = pltpu.make_async_copy(lpair, pbuf.at[1], loc_sem.at[1])
    in_lq = pltpu.make_async_copy(lq, lqv, loc_sem.at[2])
    own_q = pltpu.make_async_copy(sq.at[:, h], gq.at[own], loc_sem.at[3])
    in_sp.start()
    in_lp.start()
    in_lq.start()
    own_q.start()

    def by_head(n, store):
        for t in range(TOK // 32):
            part = pbuf[n, t].astype(F32).reshape(32 * NH, 2 * D)
            kscr[t * 32 * NH : (t + 1) * 32 * NH, :] = part[:, :D]
            vscr[t * 32 * NH : (t + 1) * 32 * NH, :] = part[:, D:]
        for c in range(NH):
            store(c, kscr[pl.ds(c, TOK, stride=NH), :].astype(BF16), vscr[pl.ds(c, TOK, stride=NH), :].astype(BF16))

    def store_short(c, k, v):
        skv[c, :, :, :D] = k.reshape(TOK // TB, TB, D)
        skv[c, :, :, D:] = v.reshape(TOK // TB, TB, D)

    def store_long(c, k, v):
        lkv[c, :, :D] = k
        lkv[c, :, D:] = v

    in_sp.wait()
    by_head(0, store_short)
    gq[NH * TOK :, :, :] = jnp.zeros((DOC, QH, D), BF16)
    gkv[NH * TOK // TB :] = jnp.zeros((KROWS // TB, TB, 2 * D), BF16)
    pl.semaphore_wait(barrier, NH - 1 + NG - 1)

    def k_copy(o):
        peer = (h + o) % NH
        return pltpu.make_async_remote_copy(
            skv.at[peer], gkv.at[own_kv], xk_send.at[o], xk_recv.at[o],
            device_id=(g, peer), device_id_type=MESH)

    def q_copy(o):
        peer = (h + o) % NH
        return pltpu.make_async_remote_copy(
            sq.at[:, peer], gq.at[own], xq_send.at[o], xq_recv.at[o],
            device_id=(g, peer), device_id_type=MESH)

    for o in range(1, NH):
        k_copy(o).start()
    for o in range(1, NH):
        q_copy(o).start()
    own_k = pltpu.make_async_copy(skv.at[h], gkv.at[own_kv], loc_sem.at[4])
    own_k.start()

    partner = h + 1 - 2 * core

    def l_copy(n):
        return pltpu.make_async_remote_copy(
            lkv, lall.at[h], l_send.at[n], l_recv.at[n],
            device_id=(g, (h + 2 * n) % NH), device_id_type=MESH)

    def f_copy(n):
        src = (h + NH - 2 * n) % NH
        return pltpu.make_async_remote_copy(
            lall.at[src], lall.at[src], f_send.at[n], f_recv.at[n],
            device_id=(g, partner), device_id_type=MESH)

    l_pair = pltpu.make_async_remote_copy(
        lkv, lall.at[h], f_send.at[0], f_recv.at[0],
        device_id=(g, partner), device_id_type=MESH)
    own_l = pltpu.make_async_copy(lkv, lall.at[h], loc_sem.at[5])

    in_lp.wait()
    by_head(1, store_long)
    l_pair.start()
    own_l.start()

    def v_copy(i):
        to, _ = group_at(i)
        return pltpu.make_async_remote_copy(
            send.at[i, pl.ds(WROWS, DOC)], recv_out.at[g, pl.ds(WROWS, DOC)], v_send.at[i], v_recv.at[i],
            device_id=(to, h), device_id_type=MESH)

    def z_copy(i):
        to, _ = group_at(i)
        return pltpu.make_async_remote_copy(
            send.at[i, pl.ds(0, WROWS)], recv_out.at[g, pl.ds(0, WROWS)], z_send.at[i], z_recv.at[i],
            device_id=(to, h), device_id_type=MESH)

    def slot_pair(i):
        to, _ = group_at(i)
        kv = gkv[pl.ds(tabs[2, to], KROWS // TB)].reshape(KROWS, 2 * D)
        pick = lax.broadcasted_iota(jnp.int32, (DOC, KROWS), 0) + tabs[3, to]
        pick = (pick == lax.broadcasted_iota(jnp.int32, (DOC, KROWS), 1)).astype(BF16)
        kv = jnp.dot(pick, kv, preferred_element_type=F32).astype(BF16)
        kslot[i] = kv[:, :D]
        send[i, WROWS:SLOT, :] = kv[:, D:]

    perm = perm_matrix()

    def slot(i):
        to, _ = group_at(i)
        q = gq[pl.ds(tabs[0, to], DOC)].astype(F32).reshape(DOC * QH, D).astype(BF16)
        for b, w in enumerate(slot_weights(q, kslot[i], tabs[1, to], perm)):
            send[i, wrow(b) : wrow(b + 1), :] = w

    own_slot = pltpu.make_async_copy(send.at[SELF], recv_out.at[g], loc_sem.at[6])

    GROUP = 4

    def in_groups(work, copy):
        def start(j):
            for d in range(GROUP):
                i = j * GROUP + d

                @pl.when(i != SELF)
                def _(i=i):
                    copy(i).start()

        def step(j):
            for d in range(GROUP):
                work(j * GROUP + d)

        step(0)

        @pl.loop(1, NG // GROUP)
        def _(j):
            step(j)
            start(j - 1)

        start(jnp.int32(NG // GROUP - 1))

    own_k.wait()
    for o in range(1, NH):
        k_copy(o).wait_recv()
    in_groups(slot_pair, v_copy)

    R = 32
    M = R * QH
    TILES = NH * TOK // R

    def long_block(n, first):
        at = 2 * (x - n)

        def tile(i, _):
            c, t = i // (TOK // R), i % (TOK // R)
            rows = pl.ds(pl.multiple_of(i * M, M), M)
            q = lqv[pl.ds(t * R, R), c].astype(F32).reshape(M, D).astype(BF16)
            k = lall[pl.ds(at, 2), c, :, 0:D].reshape(2 * TOK, D)
            v = lall[pl.ds(at, 2), c, :, D : 2 * D].reshape(2 * TOK, D)
            s = lax.dot_general(q, k, (((1,), (1,)), ((), ())), preferred_element_type=F32)
            if first:
                row = core * TOK + t * R + lax.broadcasted_iota(jnp.int32, (M, 2 * TOK), 0) // QH
                col = lax.broadcasted_iota(jnp.int32, (M, 2 * TOK), 1)
                s = jnp.where(col <= row, s, -1e30)
            top = jnp.max(jnp.maximum(s[:, :D], s[:, D:]), axis=1, keepdims=True)
            top = jnp.broadcast_to(top, (M, D))
            if not first:
                old = mx[rows, :]
                top = jnp.maximum(old, top)
                fade = jnp.exp2((old - top) * SCALE2)
            p0 = jnp.exp2((s[:, :D] - top) * SCALE2)
            p1 = jnp.exp2((s[:, D:] - top) * SCALE2)
            p = jnp.concatenate([p0.astype(BF16), p1.astype(BF16)], axis=1)
            part = jnp.dot(p, v, preferred_element_type=F32)
            mx[rows, :] = top
            if first:
                sm[rows, :] = p0 + p1
                acc[rows, :] = part
            else:
                sm[rows, :] = sm[rows, :] * fade + (p0 + p1)
                acc[rows, :] = acc[rows, :] * fade + part
            return 0

        lax.fori_loop(0, TILES, tile, 0, unroll=8)

    in_lq.wait()
    own_l.wait()
    l_pair.wait_recv()
    long_block(0, True)

    own_q.wait()
    for o in range(1, NH):
        q_copy(o).wait_recv()
    for o in range(1, NH):
        k_copy(o).wait_send()
        q_copy(o).wait_send()
    for n in range(1, 4):
        @pl.when(x + n < 4)
        def _(n=n):
            l_copy(n).start()

    in_groups(slot, z_copy)
    own_slot.start()

    @pl.loop(1, x + 1)
    def _(n):
        l_copy(n).wait_recv()
        f_copy(n).start()
        f_copy(n).wait_recv()
        long_block(n, False)

    def out_copy(c):
        return pltpu.make_async_copy(
            lout.at[c], long_out.at[:, pl.ds(pl.multiple_of(c * QH * D, QH * D), QH * D)], loc_sem.at[8 + c])

    @pl.loop(0, NH)
    def _(c):
        for t in range(TOK // R):
            rows = pl.ds(pl.multiple_of((c * (TOK // R) + t) * M, M), M)
            total = jnp.sum(sm[rows, :], axis=1, keepdims=True)
            otile[t * M : (t + 1) * M, :] = acc[rows, :] * (1.0 / total)
        for t in range(TOK // R):
            for e in range(QH):
                part = otile[pl.ds(t * M + e, R, stride=QH), :].astype(BF16)
                lout[c, t * R : (t + 1) * R, e * D : (e + 1) * D] = part
        out_copy(c).start()

    l_pair.wait_send()
    for n in range(1, 4):
        @pl.when(x + n < 4)
        def _(n=n):
            l_copy(n).wait_send()

        @pl.when(x >= n)
        def _(n=n):
            f_copy(n).wait_send()

    @pl.loop(0, NG)
    def _(i):
        @pl.when(i != SELF)
        def _():
            _, source = group_at(i)
            for lo, size, ss, rs in ((WROWS, DOC, v_send, v_recv), (0, WROWS, z_send, z_recv)):
                pltpu.make_async_remote_copy(
                    send.at[i, pl.ds(lo, size)], recv_out.at[source, pl.ds(lo, size)], ss.at[i], rs.at[i],
                    device_id=(source, h), device_id_type=MESH).wait()

    own_slot.wait()
    for c in range(NH):
        out_copy(c).wait()


def exchange(sq, spair, lq, lpair, tabs):
    any_spec = pl.BlockSpec(memory_space=pl.ANY)
    smem = pl.BlockSpec(memory_space=pltpu.SMEM)
    dma = pltpu.SemaphoreType.DMA
    return pl.pallas_call(
        main_kernel,
        out_shape=(
            jax.ShapeDtypeStruct((NG, SLOT, D), BF16),
            jax.ShapeDtypeStruct((TOK, NH * QH * D), BF16),
        ),
        in_specs=[any_spec] * 4 + [smem],
        out_specs=(any_spec, any_spec),
        scratch_shapes=[
            pltpu.VMEM((NH * TOK + DOC, QH, D), BF16),
            pltpu.VMEM(((NH * TOK + KROWS) // TB, TB, 2 * D), BF16),
            pltpu.VMEM((2, TOK // 32, 32, NH, 2 * D), BF16),
            pltpu.VMEM((NH, TOK // TB, TB, 2 * D), BF16),
            pltpu.VMEM((NH, TOK, 2 * D), BF16),
            pltpu.VMEM((TOK * NH, D), F32),
            pltpu.VMEM((TOK * NH, D), F32),
            pltpu.VMEM((NG, DOC, D), BF16),
            pltpu.VMEM((NG, SLOT, D), BF16),
            pltpu.VMEM((NH, NH, TOK, 2 * D), BF16),
            pltpu.VMEM((TOK, NH, QH, D), BF16),
            pltpu.VMEM((NH, TOK, QH * D), BF16),
            pltpu.VMEM((TOK * NH * QH, D), F32),
            pltpu.VMEM((TOK * NH * QH, D), F32),
            pltpu.VMEM((TOK * NH * QH, D), F32),
            pltpu.VMEM((TOK * QH, D), F32),
            dma((NH,)), dma((NH,)), dma((NH,)), dma((NH,)),
            dma((NG,)), dma((NG,)), dma((NG,)), dma((NG,)),
            dma((4,)), dma((4,)), dma((4,)), dma((4,)),
            dma((16,)),
        ],
        compiler_params=pltpu.CompilerParams(
            collective_id=0, has_side_effects=True, vmem_limit_bytes=48 << 20),
        name="exchange",
    )(sq, spair, lq, lpair, tabs)


def place_kernel(got, long_in, short_out, long_out, obuf, out_sem, l_sem):
    per_step = 4
    steps = NG // per_step

    def o_copy(j):
        part = pl.ds(pl.multiple_of(j * per_step * DOC, per_step * DOC), per_step * DOC)
        return pltpu.make_async_copy(obuf.at[part], short_out.at[part], out_sem.at[j])

    l_put = pltpu.make_async_copy(long_in, long_out, l_sem)

    def step(j, _):
        for d in range(per_step):
            s = j * per_step + d
            v = got[s, WROWS:SLOT, :]
            for b in range(NB):
                w = got[s, wrow(b) : wrow(b + 1), :]
                o = lax.dot_general(w, v[: TB * (b + 1)], (((0,), (0,)), ((), ())), preferred_element_type=F32)
                o = o.astype(BF16)
                rows = pl.ds(pl.multiple_of(s * DOC + b * TB, TB), TB)
                for e in range(QH):
                    obuf[rows, e * D : (e + 1) * D] = o[e * TB : (e + 1) * TB, :]
        o_copy(j).start()
        return 0

    l_put.start()
    lax.fori_loop(0, steps, step, 0)
    for j in range(steps):
        o_copy(j).wait()
    l_put.wait()


def place(got, long_in):
    any_spec = pl.BlockSpec(memory_space=pl.ANY)
    dma = pltpu.SemaphoreType.DMA
    return pl.pallas_call(
        place_kernel,
        out_shape=(
            jax.ShapeDtypeStruct((NG * DOC, QH * D), BF16),
            jax.ShapeDtypeStruct((TOK, NH * QH * D), BF16),
        ),
        in_specs=[pl.BlockSpec(memory_space=pltpu.VMEM), any_spec],
        out_specs=(any_spec, any_spec),
        scratch_shapes=[
            pltpu.VMEM((NG * DOC, QH * D), BF16),
            dma((8,)), dma,
        ],
        compiler_params=pltpu.CompilerParams(vmem_limit_bytes=24 << 20),
        name="place",
    )(got, long_in)


def slot_tables(doc_lengths, destinations):
    g = lax.axis_index("grp")
    lens = lax.dynamic_index_in_dim(doc_lengths, g, 0, keepdims=False)
    dest = lax.dynamic_index_in_dim(destinations, g, 0, keepdims=False)
    doc = jnp.arange(NG, dtype=jnp.int32)
    hit = dest[None, :] == doc[:, None]
    before = jnp.where(doc[None, :] < doc[:, None], lens[None, :], 0).sum(axis=1)
    start = jnp.where(hit, before[None, :], 0).sum(axis=1)
    rows = jnp.where(hit, lens[None, :], 0).sum(axis=1)
    return jnp.stack([start, rows, start // TB, start % TB])


def on_device(long_queries, long_pairs, short_queries, short_pairs, doc_lengths, destinations):
    queries = (TOK, NH, QH, D)
    pairs = (TOK // 32, 32, NH, 2 * D)

    def stay(array, shape):
        return pltpu.with_memory_space_constraint(array.reshape(shape), pltpu.HBM)

    got, long_mix = exchange(
        stay(short_queries, queries),
        stay(short_pairs, pairs),
        stay(long_queries, queries),
        stay(long_pairs, pairs),
        slot_tables(doc_lengths, destinations),
    )
    short_placed, long_result = place(got, long_mix)
    return long_result, short_placed


def solution(mesh):
    rows = P(("grp", "head"), None, None)
    return jax.shard_map(
        on_device,
        mesh=mesh,
        in_specs=(rows, rows, rows, rows, P(), P()),
        out_specs=(P(("grp", "head"), None), P("grp", "head")),
        check_vma=False,
    )
```

```python
import functools
import math

import jax
import jax.numpy as jnp
from jax import lax
from jax.experimental import pallas as pl
from jax.experimental.pallas import tpu as pltpu
from jax.sharding import PartitionSpec as P

MESH = pl.DeviceIdType.MESH
BF16 = jnp.bfloat16
F32 = jnp.float32

NG = 32
NH = 8
TOK = 128
QH = 8
D = 128
DOC = 64
TB = 16
NB = DOC // TB
WROWS = TB * NB * (NB + 1) // 2
SLOT = WROWS + DOC
KROWS = DOC + TB
SCALE2 = math.log2(math.e) / math.sqrt(D)


def wrow(block):
    return TB * block * (block + 1) // 2


def perm_matrix():
    row = lax.broadcasted_iota(jnp.int32, (D, D), 0)
    col = lax.broadcasted_iota(jnp.int32, (D, D), 1)
    return (col == (row % QH) * TB + row // QH).astype(BF16)


def slot_weights(q, k, length, perm):
    st = lax.dot_general(k, q, (((1,), (1,)), ((), ())), preferred_element_type=F32)
    out = []
    for b in range(NB):
        keys = TB * (b + 1)
        s = st[:keys, b * D : (b + 1) * D]
        key = lax.broadcasted_iota(jnp.int32, (keys, D), 0)
        tok = TB * b + lax.broadcasted_iota(jnp.int32, (keys, D), 1) // QH
        s = jnp.where(key <= tok, s, -1e30)
        top = jnp.max(s, axis=0, keepdims=True)
        p = jnp.exp2((s - top) * SCALE2)
        inv = 1.0 / jnp.sum(p, axis=0, keepdims=True)
        inv = jnp.where(tok[:1] < length, inv, 0.0)
        w = (p * inv).astype(BF16)
        w = jnp.dot(w, perm, preferred_element_type=F32).astype(BF16)
        out.append(w)
    return out


def main_kernel(
    sq, spair, lq, lpair, tabs,
    recv_out, long_out,
    gq, gkv, pbuf, skv, lkv, kscr, vscr, kslot, send, lall, lqv, lout, acc, mx, sm, otile,
    xq_send, xq_recv, xk_send, xk_recv, z_send, z_recv, v_send, v_recv,
    l_send, l_recv, f_send, f_recv, loc_sem,
):
    g = lax.axis_index("grp")
    h = lax.axis_index("head")
    y, z = g // 8, g % 8
    x, core = h // 2, h % 2

    def group_at(i):
        m = i % 8
        oz = jnp.where(m % 2 == 0, m // 2 + 1, 8 - (m // 2 + 1))
        oz = jnp.where(m == 7, 0, oz)
        oy = i // 8
        return ((y + oy) % 4) * 8 + (z + oz) % 8, ((y + 4 - oy) % 4) * 8 + (z + 8 - oz) % 8

    SELF = 7

    barrier = pltpu.get_barrier_semaphore()

    @pl.loop(1, NG)
    def _(o):
        pl.semaphore_signal(barrier, inc=1, device_id=((g + o) % NG, h), device_id_type=MESH)

    for o in range(1, NH):
        pl.semaphore_signal(barrier, inc=1, device_id=(g, (h + o) % NH), device_id_type=MESH)

    own = pl.ds(pl.multiple_of(h * TOK, TOK), TOK)
    own_kv = pl.ds(h * (TOK // TB), TOK // TB)
    in_sp = pltpu.make_async_copy(spair, pbuf.at[0], loc_sem.at[0])
    in_lp = pltpu.make_async_copy(lpair, pbuf.at[1], loc_sem.at[1])
    in_lq = pltpu.make_async_copy(lq, lqv, loc_sem.at[2])
    own_q = pltpu.make_async_copy(sq.at[:, h], gq.at[own], loc_sem.at[3])
    in_sp.start()
    in_lp.start()
    in_lq.start()
    own_q.start()

    def by_head(n, store):
        for t in range(TOK // 32):
            part = pbuf[n, t].astype(F32).reshape(32 * NH, 2 * D)
            kscr[t * 32 * NH : (t + 1) * 32 * NH, :] = part[:, :D]
            vscr[t * 32 * NH : (t + 1) * 32 * NH, :] = part[:, D:]
        for c in range(NH):
            store(c, kscr[pl.ds(c, TOK, stride=NH), :].astype(BF16), vscr[pl.ds(c, TOK, stride=NH), :].astype(BF16))

    def store_short(c, k, v):
        skv[c, :, :, :D] = k.reshape(TOK // TB, TB, D)
        skv[c, :, :, D:] = v.reshape(TOK // TB, TB, D)

    def store_long(c, k, v):
        lkv[c, :, :D] = k
        lkv[c, :, D:] = v

    in_sp.wait()
    by_head(0, store_short)
    gq[NH * TOK :, :, :] = jnp.zeros((DOC, QH, D), BF16)
    gkv[NH * TOK // TB :] = jnp.zeros((KROWS // TB, TB, 2 * D), BF16)
    pl.semaphore_wait(barrier, NH - 1 + NG - 1)

    def k_copy(o):
        peer = (h + o) % NH
        return pltpu.make_async_remote_copy(
            skv.at[peer], gkv.at[own_kv], xk_send.at[o], xk_recv.at[o],
            device_id=(g, peer), device_id_type=MESH)

    def q_copy(o):
        peer = (h + o) % NH
        return pltpu.make_async_remote_copy(
            sq.at[:, peer], gq.at[own], xq_send.at[o], xq_recv.at[o],
            device_id=(g, peer), device_id_type=MESH)

    for o in range(1, NH):
        k_copy(o).start()
    for o in range(1, NH):
        q_copy(o).start()
    own_k = pltpu.make_async_copy(skv.at[h], gkv.at[own_kv], loc_sem.at[4])
    own_k.start()

    partner = h + 1 - 2 * core

    def l_copy(n):
        return pltpu.make_async_remote_copy(
            lkv, lall.at[h], l_send.at[n], l_recv.at[n],
            device_id=(g, (h + 2 * n) % NH), device_id_type=MESH)

    def f_copy(n):
        src = (h + NH - 2 * n) % NH
        return pltpu.make_async_remote_copy(
            lall.at[src], lall.at[src], f_send.at[n], f_recv.at[n],
            device_id=(g, partner), device_id_type=MESH)

    l_pair = pltpu.make_async_remote_copy(
        lkv, lall.at[h], f_send.at[0], f_recv.at[0],
        device_id=(g, partner), device_id_type=MESH)
    own_l = pltpu.make_async_copy(lkv, lall.at[h], loc_sem.at[5])

    in_lp.wait()
    by_head(1, store_long)
    l_pair.start()
    own_l.start()

    def v_copy(i):
        to, _ = group_at(i)
        return pltpu.make_async_remote_copy(
            send.at[i, pl.ds(WROWS, DOC)], recv_out.at[g, pl.ds(WROWS, DOC)], v_send.at[i], v_recv.at[i],
            device_id=(to, h), device_id_type=MESH)

    def z_copy(i):
        to, _ = group_at(i)
        return pltpu.make_async_remote_copy(
            send.at[i, pl.ds(0, WROWS)], recv_out.at[g, pl.ds(0, WROWS)], z_send.at[i], z_recv.at[i],
            device_id=(to, h), device_id_type=MESH)

    def slot_pair(i):
        to, _ = group_at(i)
        kv = gkv[pl.ds(tabs[2, to], KROWS // TB)].reshape(KROWS, 2 * D)
        pick = lax.broadcasted_iota(jnp.int32, (DOC, KROWS), 0) + tabs[3, to]
        pick = (pick == lax.broadcasted_iota(jnp.int32, (DOC, KROWS), 1)).astype(BF16)
        kv = jnp.dot(pick, kv, preferred_element_type=F32).astype(BF16)
        kslot[i] = kv[:, :D]
        send[i, WROWS:SLOT, :] = kv[:, D:]

    perm = perm_matrix()

    def slot(i):
        to, _ = group_at(i)
        q = gq[pl.ds(tabs[0, to], DOC)].astype(F32).reshape(DOC * QH, D).astype(BF16)
        for b, w in enumerate(slot_weights(q, kslot[i], tabs[1, to], perm)):
            send[i, wrow(b) : wrow(b + 1), :] = w

    own_slot = pltpu.make_async_copy(send.at[SELF], recv_out.at[g], loc_sem.at[6])

    GROUP = 4

    def in_groups(work, copy):
        def start(j):
            for d in range(GROUP):
                i = j * GROUP + d

                @pl.when(i != SELF)
                def _(i=i):
                    copy(i).start()

        def step(j):
            for d in range(GROUP):
                work(j * GROUP + d)

        step(0)

        @pl.loop(1, NG // GROUP)
        def _(j):
            step(j)
            start(j - 1)

        start(jnp.int32(NG // GROUP - 1))

    own_k.wait()
    for o in range(1, NH):
        k_copy(o).wait_recv()
    in_groups(slot_pair, v_copy)

    R = 32
    M = R * QH
    TILES = NH * TOK // R

    def long_block(n, first):
        at = 2 * (x - n)

        def tile(i, _):
            c, t = i // (TOK // R), i % (TOK // R)
            rows = pl.ds(pl.multiple_of(i * M, M), M)
            q = lqv[pl.ds(t * R, R), c].astype(F32).reshape(M, D).astype(BF16)
            k = lall[pl.ds(at, 2), c, :, 0:D].reshape(2 * TOK, D)
            v = lall[pl.ds(at, 2), c, :, D : 2 * D].reshape(2 * TOK, D)
            s = lax.dot_general(q, k, (((1,), (1,)), ((), ())), preferred_element_type=F32)
            if first:
                row = core * TOK + t * R + lax.broadcasted_iota(jnp.int32, (M, 2 * TOK), 0) // QH
                col = lax.broadcasted_iota(jnp.int32, (M, 2 * TOK), 1)
                s = jnp.where(col <= row, s, -1e30)
            top = jnp.max(jnp.maximum(s[:, :D], s[:, D:]), axis=1, keepdims=True)
            top = jnp.broadcast_to(top, (M, D))
            if not first:
                old = mx[rows, :]
                top = jnp.maximum(old, top)
                fade = jnp.exp2((old - top) * SCALE2)
            p0 = jnp.exp2((s[:, :D] - top) * SCALE2)
            p1 = jnp.exp2((s[:, D:] - top) * SCALE2)
            p = jnp.concatenate([p0.astype(BF16), p1.astype(BF16)], axis=1)
            part = jnp.dot(p, v, preferred_element_type=F32)
            mx[rows, :] = top
            if first:
                sm[rows, :] = p0 + p1
                acc[rows, :] = part
            else:
                sm[rows, :] = sm[rows, :] * fade + (p0 + p1)
                acc[rows, :] = acc[rows, :] * fade + part
            return 0

        lax.fori_loop(0, TILES, tile, 0, unroll=8)

    in_lq.wait()
    own_l.wait()
    l_pair.wait_recv()
    long_block(0, True)

    own_q.wait()
    for o in range(1, NH):
        q_copy(o).wait_recv()
    for n in range(1, 4):
        @pl.when(x + n < 4)
        def _(n=n):
            l_copy(n).start()

    in_groups(slot, z_copy)
    own_slot.start()

    @pl.loop(1, x + 1)
    def _(n):
        l_copy(n).wait_recv()
        f_copy(n).start()
        f_copy(n).wait_recv()
        long_block(n, False)

    def out_copy(c):
        return pltpu.make_async_copy(
            lout.at[c], long_out.at[:, pl.ds(pl.multiple_of(c * QH * D, QH * D), QH * D)], loc_sem.at[8 + c])

    @pl.loop(0, NH)
    def _(c):
        for t in range(TOK // R):
            rows = pl.ds(pl.multiple_of((c * (TOK // R) + t) * M, M), M)
            total = jnp.sum(sm[rows, :], axis=1, keepdims=True)
            otile[t * M : (t + 1) * M, :] = acc[rows, :] * (1.0 / total)
        for t in range(TOK // R):
            for e in range(QH):
                part = otile[pl.ds(t * M + e, R, stride=QH), :].astype(BF16)
                lout[c, t * R : (t + 1) * R, e * D : (e + 1) * D] = part
        out_copy(c).start()

    for o in range(1, NH):
        k_copy(o).wait_send()
        q_copy(o).wait_send()
    l_pair.wait_send()
    for n in range(1, 4):
        @pl.when(x + n < 4)
        def _(n=n):
            l_copy(n).wait_send()

        @pl.when(x >= n)
        def _(n=n):
            f_copy(n).wait_send()

    @pl.loop(0, NG)
    def _(i):
        @pl.when(i != SELF)
        def _():
            _, source = group_at(i)
            for lo, size, ss, rs in ((WROWS, DOC, v_send, v_recv), (0, WROWS, z_send, z_recv)):
                pltpu.make_async_remote_copy(
                    send.at[i, pl.ds(lo, size)], recv_out.at[source, pl.ds(lo, size)], ss.at[i], rs.at[i],
                    device_id=(source, h), device_id_type=MESH).wait()

    own_slot.wait()
    for c in range(NH):
        out_copy(c).wait()


def exchange(sq, spair, lq, lpair, tabs):
    any_spec = pl.BlockSpec(memory_space=pl.ANY)
    smem = pl.BlockSpec(memory_space=pltpu.SMEM)
    dma = pltpu.SemaphoreType.DMA
    return pl.pallas_call(
        main_kernel,
        out_shape=(
            jax.ShapeDtypeStruct((NG, SLOT, D), BF16),
            jax.ShapeDtypeStruct((TOK, NH * QH * D), BF16),
        ),
        in_specs=[any_spec] * 4 + [smem],
        out_specs=(any_spec, any_spec),
        scratch_shapes=[
            pltpu.VMEM((NH * TOK + DOC, QH, D), BF16),
            pltpu.VMEM(((NH * TOK + KROWS) // TB, TB, 2 * D), BF16),
            pltpu.VMEM((2, TOK // 32, 32, NH, 2 * D), BF16),
            pltpu.VMEM((NH, TOK // TB, TB, 2 * D), BF16),
            pltpu.VMEM((NH, TOK, 2 * D), BF16),
            pltpu.VMEM((TOK * NH, D), F32),
            pltpu.VMEM((TOK * NH, D), F32),
            pltpu.VMEM((NG, DOC, D), BF16),
            pltpu.VMEM((NG, SLOT, D), BF16),
            pltpu.VMEM((NH, NH, TOK, 2 * D), BF16),
            pltpu.VMEM((TOK, NH, QH, D), BF16),
            pltpu.VMEM((NH, TOK, QH * D), BF16),
            pltpu.VMEM((TOK * NH * QH, D), F32),
            pltpu.VMEM((TOK * NH * QH, D), F32),
            pltpu.VMEM((TOK * NH * QH, D), F32),
            pltpu.VMEM((TOK * QH, D), F32),
            dma((NH,)), dma((NH,)), dma((NH,)), dma((NH,)),
            dma((NG,)), dma((NG,)), dma((NG,)), dma((NG,)),
            dma((4,)), dma((4,)), dma((4,)), dma((4,)),
            dma((16,)),
        ],
        compiler_params=pltpu.CompilerParams(
            collective_id=0, has_side_effects=True, vmem_limit_bytes=48 << 20),
        name="exchange",
    )(sq, spair, lq, lpair, tabs)


def place_kernel(got, long_in, short_out, long_out, obuf, out_sem, l_sem):
    per_step = 4
    steps = NG // per_step

    def o_copy(j):
        part = pl.ds(pl.multiple_of(j * per_step * DOC, per_step * DOC), per_step * DOC)
        return pltpu.make_async_copy(obuf.at[part], short_out.at[part], out_sem.at[j])

    l_put = pltpu.make_async_copy(long_in, long_out, l_sem)

    def step(j, _):
        for d in range(per_step):
            s = j * per_step + d
            v = got[s, WROWS:SLOT, :]
            for b in range(NB):
                w = got[s, wrow(b) : wrow(b + 1), :]
                o = lax.dot_general(w, v[: TB * (b + 1)], (((0,), (0,)), ((), ())), preferred_element_type=F32)
                o = o.astype(BF16)
                rows = pl.ds(pl.multiple_of(s * DOC + b * TB, TB), TB)
                for e in range(QH):
                    obuf[rows, e * D : (e + 1) * D] = o[e * TB : (e + 1) * TB, :]
        o_copy(j).start()
        return 0

    l_put.start()
    lax.fori_loop(0, steps, step, 0)
    for j in range(steps):
        o_copy(j).wait()
    l_put.wait()


def place(got, long_in):
    any_spec = pl.BlockSpec(memory_space=pl.ANY)
    dma = pltpu.SemaphoreType.DMA
    return pl.pallas_call(
        place_kernel,
        out_shape=(
            jax.ShapeDtypeStruct((NG * DOC, QH * D), BF16),
            jax.ShapeDtypeStruct((TOK, NH * QH * D), BF16),
        ),
        in_specs=[pl.BlockSpec(memory_space=pltpu.VMEM), any_spec],
        out_specs=(any_spec, any_spec),
        scratch_shapes=[
            pltpu.VMEM((NG * DOC, QH * D), BF16),
            dma((8,)), dma,
        ],
        compiler_params=pltpu.CompilerParams(vmem_limit_bytes=24 << 20),
        name="place",
    )(got, long_in)


def slot_tables(doc_lengths, destinations):
    g = lax.axis_index("grp")
    lens = lax.dynamic_index_in_dim(doc_lengths, g, 0, keepdims=False)
    dest = lax.dynamic_index_in_dim(destinations, g, 0, keepdims=False)
    doc = jnp.arange(NG, dtype=jnp.int32)
    hit = dest[None, :] == doc[:, None]
    before = jnp.where(doc[None, :] < doc[:, None], lens[None, :], 0).sum(axis=1)
    start = jnp.where(hit, before[None, :], 0).sum(axis=1)
    rows = jnp.where(hit, lens[None, :], 0).sum(axis=1)
    return jnp.stack([start, rows, start // TB, start % TB])


def on_device(long_queries, long_pairs, short_queries, short_pairs, doc_lengths, destinations):
    queries = (TOK, NH, QH, D)
    pairs = (TOK // 32, 32, NH, 2 * D)

    def stay(array, shape):
        return pltpu.with_memory_space_constraint(array.reshape(shape), pltpu.HBM)

    got, long_mix = exchange(
        stay(short_queries, queries),
        stay(short_pairs, pairs),
        stay(long_queries, queries),
        stay(long_pairs, pairs),
        slot_tables(doc_lengths, destinations),
    )
    short_placed, long_result = place(got, long_mix)
    return long_result, short_placed


def solution(mesh):
    rows = P(("grp", "head"), None, None)
    return jax.shard_map(
        on_device,
        mesh=mesh,
        in_specs=(rows, rows, rows, rows, P(), P()),
        out_specs=(P(("grp", "head"), None), P("grp", "head")),
        check_vma=False,
    )
```
